256 devices in a mesh: energy: 128 (over z_lo, x, y, core), mom: 2 (over z_hi).
Axes of the slice: x: 4, y: 4, z: 8 (z_hi: 2, z_lo: 4; z = z_hi * 4 + z_lo), core: 2. Of those that a mesh axis runs over, the one named last changes fastest.
Arguments:
- system_matrix: float32 [2, 128, 4, 384, 384], P(None, 'energy', 'mom'), may hold values from -1 to 5
- approx_inverse: float32 [2, 128, 4, 384], P(None, 'energy', 'mom'), may hold values from -1.2 to 1.2
- mode_weight: float32 [4, 6], replicated, may hold values from 0.05 to 0.3
- phonon_shift: int32 [4, 6], replicated, may hold values from -8 to 8
- pairing: int32 [4, 4], replicated, may hold values from 0 to 3
- coupling: float32 [384, 384], P('energy'), may hold values from 0.3 to 1.5
- energy_weight: float32 [128], P('energy'), may hold values from 0.5 to 2
- force_weight: float32 [384, 384], P('energy'), may hold values from -0.25 to 0.25
Outputs:
- green: float32 [2, 128, 4, 384, 384], P(None, 'energy', 'mom')
- sigma: float32 [2, 128, 4, 384, 384], P(None, 'energy', 'mom')
- force: float32 [384, 384], P('energy')
The draws below stay inside these ranges and needn't reach their ends.
All inputs are finite; a program needn't handle non-finite values.
Results may differ from the reference program's by a relative error of at most 0.0001.
Values sent between devices are 32-bit elements; how exact they have to be, the bound alone decides.
A program may use at most 128 MiB of HBM per device.

```python
import math
import jax
import jax.numpy as jnp
from jax import lax

B = 384
NMODE = 6
SMAX = 8
NE = 128
NK = 4
NQ = 4


def diagonal_parts(key):
    base = jax.random.fold_in(key, 11)
    first, second, third = jax.random.split(base, 3)
    real_diag = 4.0 ** jax.random.uniform(first, (NE, NK, B), jnp.float32)
    imag_diag = jax.random.uniform(second, (NE, NK, B), jnp.float32, 0.1, 0.5)
    factor = 1.0 + jax.random.uniform(third, (NE, NK, B), jnp.float32, -0.2, 0.2)
    return (real_diag, imag_diag, factor)


def draw_system_matrix(key, part):
    real_diag, imag_diag, factor = diagonal_parts(key)
    noise_key = jax.random.fold_in(key, 23)
    noise = jnp.clip(jax.random.normal(noise_key, (2, NE, NK, B, B), jnp.float32) * 0.7071, -2.8, 2.8)
    scale = 0.7 / math.sqrt(B) * jnp.sqrt(real_diag[..., :, None] * real_diag[..., None, :])
    identity = jnp.eye(B, dtype=jnp.float32)
    real_part = noise[0] * scale + identity * real_diag[..., None]
    imag_part = noise[1] * scale + identity * imag_diag[..., None]
    return jnp.stack([real_part, imag_part])


def draw_approx_inverse(key, part):
    real_diag, imag_diag, factor = diagonal_parts(key)
    denom = real_diag * real_diag + imag_diag * imag_diag
    return jnp.stack([factor * real_diag / denom, -factor * imag_diag / denom])


def place_ends(result, rng, smallest, largest):
    place = [jax.random.randint(jax.random.fold_in(rng, axis), (), 0, length) for axis, length in enumerate(result.shape)]
    widest = result.shape.index(max(result.shape))
    next_to = place[:widest] + [(place[widest] + 1) % result.shape[widest]] + place[widest + 1:]
    return result.at[tuple(place)].set(smallest).at[tuple(next_to)].set(largest)


def level_of(key, shape, cuts, smallest, high):
    factor_of = 1.0
    for dim, shards_of in cuts:
        heights = jax.random.uniform(jax.random.fold_in(jax.random.fold_in(key, 6), dim), (shards_of,), jnp.float32, smallest / len(cuts), high / len(cuts))
        factor_of = factor_of * jnp.repeat(jnp.exp(heights), shape[dim] // shards_of).reshape((-1,) + (1,) * (len(shape) - 1 - dim))
    return factor_of


def bell_draw(key, shape, deviation, reach, shards=(), kind=jnp.bfloat16):
    array = jax.random.normal(key, shape, jnp.float32) * deviation
    if len(shards) > 0:
        array = level_of(key, shape, shards, -0.22, 0.18) * array
    return jnp.clip(array, min=-reach, max=reach).astype(kind)


def setup_inputs(seed: int = 0) -> dict:
    key_of = jax.random.split(jax.random.key(seed), 9)
    return {
        "system_matrix": draw_system_matrix(jax.random.fold_in(key_of[8], 71), 0),
        "approx_inverse": draw_approx_inverse(jax.random.fold_in(key_of[8], 71), 0),
        "mode_weight": jnp.clip(jnp.exp(jax.random.uniform(key_of[2], (NQ, NMODE), jnp.float32, math.log(0.05), math.log(0.3))), 0.05, 0.3),
        "phonon_shift": place_ends(jax.random.randint(key_of[3], (NQ, NMODE), -SMAX, SMAX + 1), jax.random.fold_in(key_of[3], 1), -SMAX, SMAX).astype(jnp.int32),
        "pairing": place_ends(jax.random.randint(key_of[4], (NK, NQ), 0, NK), jax.random.fold_in(key_of[4], 1), 0, NK - 1).astype(jnp.int32),
        "coupling": jnp.clip(jnp.exp(math.log(1.5) - 1.60943787 * jax.random.uniform(key_of[5], (B, B), jnp.float32) ** level_of(key_of[5], (B, B), ((0, 128),), -0.2, 0.2)), 0.3, 1.5),
        "energy_weight": jnp.clip(jnp.exp(math.log(2.0) - 1.3862944 * jax.random.uniform(key_of[6], (NE,), jnp.float32) ** level_of(key_of[6], (NE,), ((0, 128),), -0.2, 0.2)), 0.5, 2.0),
        "force_weight": bell_draw(key_of[7], (B, B), (NE * NK) ** -0.5, 0.25, ((0, 128),), jnp.float32),
    }


highest = lax.Precision.HIGHEST


def matrix_product(left, right):
    return jnp.einsum('...ij,...jk->...ik', left, right, precision=highest, preferred_element_type=jnp.float32)


def complex_product(left_real, left_imag, right_real, right_imag):
    real_out = matrix_product(left_real, right_real) - matrix_product(left_imag, right_imag)
    imag_out = matrix_product(left_real, right_imag) + matrix_product(left_imag, right_real)
    return real_out, imag_out


def newton(matrix, approx):
    mat_real = matrix[0]
    mat_imag = matrix[1]
    diag_real = approx[0]
    diag_imag = approx[1]
    left_real = diag_real[..., :, None] * mat_real - diag_imag[..., :, None] * mat_imag
    left_imag = diag_real[..., :, None] * mat_imag + diag_imag[..., :, None] * mat_real
    both_real = left_real * diag_real[..., None, :] - left_imag * diag_imag[..., None, :]
    both_imag = left_real * diag_imag[..., None, :] + left_imag * diag_real[..., None, :]
    identity = jnp.eye(matrix.shape[-1], dtype=jnp.float32)
    iter_real = 2.0 * identity * diag_real[..., :, None] - both_real
    iter_imag = 2.0 * identity * diag_imag[..., :, None] - both_imag
    for step in range(2):
        prod_real, prod_imag = complex_product(mat_real, mat_imag, iter_real, iter_imag)
        back_real, back_imag = complex_product(iter_real, iter_imag, prod_real, prod_imag)
        iter_real = 2.0 * iter_real - back_real
        iter_imag = 2.0 * iter_imag - back_imag
    return jnp.stack([iter_real, iter_imag])


def build_kernel(phonon_shift, mode_weight, pairing, energies, momenta):
    energy_index = jnp.arange(energies, dtype=jnp.int32)
    target = energy_index[None, None, :] - phonon_shift[:, :, None]
    onehot = (target[..., None] == energy_index[None, None, None, :]).astype(jnp.float32)
    shifted = jnp.einsum('qm,qmef->qef', mode_weight, onehot, precision=highest)
    momentum_index = jnp.arange(momenta, dtype=jnp.int32)
    select = (jnp.transpose(pairing)[:, :, None] == momentum_index[None, None, :]).astype(jnp.float32)
    return jnp.einsum('qef,qkl->ekfl', shifted, select, precision=highest)


def reference(system_matrix, approx_inverse, mode_weight, phonon_shift, pairing, coupling, energy_weight, force_weight):
    def one_energy(pair):
        return newton(pair[0], pair[1])

    stacked = lax.map(one_energy, (jnp.moveaxis(system_matrix, 1, 0), jnp.moveaxis(approx_inverse, 1, 0)))
    green = jnp.moveaxis(stacked, 0, 1)
    kernel = build_kernel(phonon_shift, mode_weight, pairing, NE, NK)
    flat = kernel.reshape(NE * NK, NE * NK)
    conv = jnp.einsum('ab,cbx->cax', flat, green.reshape(2, NE * NK, B * B), precision=highest)
    sigma = conv.reshape(green.shape) * coupling
    weighted = green * energy_weight[None, :, None, None, None]
    term = jnp.einsum('akij,akjl->il', weighted[0], sigma[0], precision=highest)
    term = term - jnp.einsum('akij,akjl->il', weighted[1], sigma[1], precision=highest)
    force = force_weight * term
    return green, sigma, force
```

```python
import functools

import jax
import jax.numpy as jnp
from jax import lax
from jax.experimental import pallas as pl
from jax.experimental.pallas import tpu as pltpu
from jax.sharding import Mesh
from jax.sharding import PartitionSpec as P

AXES = ("zl", "x", "y", "c", "zh")
ENERGY = ("zl", "x", "y", "c")
MESH_ID = pl.DeviceIdType.MESH
F32 = jnp.float32
BF16 = jnp.bfloat16
B = 384
T = 3
VMEM = pl.BlockSpec(memory_space=pltpu.VMEM)
SMEM = pl.BlockSpec(memory_space=pltpu.SMEM)


def split(x):
    hi = x.astype(BF16)
    lo = (x - hi.astype(F32)).astype(BF16)
    return hi, lo


def put_left(ref, real, imag, row):
    rows = pl.ds(row, B)
    for col, part in ((0, real), (B, imag)):
        hi, lo = split(part)
        ref[rows, pl.ds(col, B)] = hi
        ref[rows, pl.ds(2 * B + col, B)] = hi
        ref[rows, pl.ds(4 * B + col, B)] = lo


def put_right(ref, real, imag):
    rh, rl = split(real)
    ih, il = split(imag)
    for base, r, i in ((0, rh, ih), (2 * B, rl, il), (4 * B, rh, ih)):
        ref[pl.ds(base, B), pl.ds(0, B)] = r
        ref[pl.ds(base, B), pl.ds(B, B)] = i
        ref[pl.ds(base + B, B), pl.ds(0, B)] = -i
        ref[pl.ds(base + B, B), pl.ds(B, B)] = r


def newton_kernel(m_ref, c_ref, g_ref, lin_ref, left, right, xr, xi):
    k = pl.program_id(0)
    row = lax.broadcasted_iota(jnp.int32, (B, B), 0)
    col = lax.broadcasted_iota(jnp.int32, (B, B), 1)
    eye = row == col
    one = jnp.where(eye, 1.0, 0.0).astype(F32)
    cr = c_ref[0, pl.ds(k, 1), :]
    ci = c_ref[1, pl.ds(k, 1), :]
    cr_col = jnp.sum(jnp.where(eye, cr, 0.0), axis=1, keepdims=True)
    ci_col = jnp.sum(jnp.where(eye, ci, 0.0), axis=1, keepdims=True)
    mr = m_ref[0, 0, 0]
    mi = m_ref[1, 0, 0]
    yr = one - (mr * cr - mi * ci)
    yi = -(mr * ci + mi * cr)
    put_left(left, yr, yi, 0)
    put_right(right, yr, yi)
    ar = one + yr
    xr[...] = cr_col * ar - ci_col * yi
    xi[...] = cr_col * yi + ci_col * ar
    y0 = jnp.dot(left[pl.ds(0, B), :], right[...], preferred_element_type=F32)
    put_left(left, y0[:, :B], y0[:, B:], B)
    put_left(left, xr[...], xi[...], 0)
    put_right(right, y0[:, :B], y0[:, B:])
    both = jnp.dot(left[...], right[...], preferred_element_type=F32)
    x1r = xr[...] + both[:B, :B]
    x1i = xi[...] + both[:B, B:]
    xr[...] = x1r
    xi[...] = x1i
    put_left(left, x1r, x1i, 0)
    put_right(right, both[B:, :B], both[B:, B:])
    last = jnp.dot(left[pl.ds(0, B), :], right[...], preferred_element_type=F32)
    for part, (ref, off) in enumerate(((xr, 0), (xi, B))):
        out = ref[...] + last[:, off : off + B]
        g_ref[part, 0, 0] = out
        for t in range(T):
            lin_ref[0, t, part] = out[:, 128 * t : 128 * (t + 1)]


def newton(matrix, approx):
    return pl.pallas_call(
        newton_kernel,
        grid=(2,),
        out_shape=(
            jax.ShapeDtypeStruct((2, 1, 2, B, B), F32),
            jax.ShapeDtypeStruct((2, T, 2, B, 128), F32),
        ),
        in_specs=[
            pl.BlockSpec((2, 1, 1, B, B), lambda k: (0, 0, k, 0, 0)),
            pl.BlockSpec((2, 2, B), lambda k: (0, 0, 0)),
        ],
        out_specs=(
            pl.BlockSpec((2, 1, 1, B, B), lambda k: (0, 0, k, 0, 0)),
            pl.BlockSpec((1, T, 2, B, 128), lambda k: (k, 0, 0, 0, 0)),
        ),
        scratch_shapes=[
            pltpu.VMEM((2 * B, 6 * B), BF16),
            pltpu.VMEM((6 * B, 2 * B), BF16),
            pltpu.VMEM((B, B), F32),
            pltpu.VMEM((B, B), F32),
        ],
        compiler_params=pltpu.CompilerParams(vmem_limit_bytes=40 << 20),
        name="newton",
    )(matrix, approx)


def here():
    return {a: lax.axis_index(a) for a in AXES}


def ring_z(me, d):
    z = lax.rem(me["zh"] * 4 + me["zl"] + d, 8)
    return z, (lax.rem(z, 4), me["x"], me["y"], me["c"], z // 4)


def plane(me, i):
    x = lax.rem(me["x"] + i // 8, 4)
    y = lax.rem(me["y"] + lax.rem(i // 2, 4), 4)
    c = lax.rem(me["c"] + lax.rem(i, 2), 2)
    return (x * 4 + y) * 2 + c, (me["zl"], x, y, c, me["zh"])


def greet(me):
    barrier = pltpu.get_barrier_semaphore()

    def along_z(d, carry):
        pl.semaphore_signal(barrier, inc=1, device_id=ring_z(me, d)[1], device_id_type=MESH_ID)
        return carry

    def in_plane(i, carry):
        pl.semaphore_signal(barrier, inc=1, device_id=plane(me, i)[1], device_id_type=MESH_ID)
        return carry

    lax.fori_loop(1, 8, along_z, 0)
    lax.fori_loop(1, 32, in_plane, 0)
    pl.semaphore_wait(barrier, 38)


def send(src, dst, ssem, rsem, device):
    pltpu.make_async_remote_copy(
        src_ref=src, dst_ref=dst, send_sem=ssem, recv_sem=rsem, device_id=device, device_id_type=MESH_ID
    ).start()


def wait_for(ref, sem):
    pltpu.make_async_copy(ref, ref, sem).wait()


def exchange_kernel(
    lin, weight, shift, pairing, coupling, out,
    zb, pb, cb, rb, kmat, shifted, xs,
    zs, zr, ps, pr, bs, br, ws, wr,
):
    me = here()
    my_z = me["zh"] * 4 + me["zl"]
    my_p = (me["x"] * 4 + me["y"]) * 2 + me["c"]
    mine = pl.ds(3 * my_p, 3)
    greet(me)

    for k in range(2):
        for t in range(T):

            def along_z(d, carry, k=k, t=t):
                z, device = ring_z(me, d)
                rows = pl.ds(pl.multiple_of(96 * lax.rem(z, 4), 8), 96)
                send(lin.at[k, t, z // 4, rows], zb.at[k, t, my_z], zs.at[k, t], zr.at[k, t], device)
                return carry

            lax.fori_loop(1, 8, along_z, 0)
            rows = pl.ds(pl.multiple_of(96 * me["zl"], 8), 96)
            pltpu.make_async_copy(lin.at[k, t, me["zh"], rows], zb.at[k, t, my_z], zr.at[k, t]).start()

    e = lax.broadcasted_iota(jnp.int32, (128, 128), 0)
    f = lax.broadcasted_iota(jnp.int32, (128, 128), 1)
    for q in range(4):
        total = jnp.zeros((128, 128), F32)
        for m in range(6):
            total = total + jnp.where(f == e - shift[q, m], weight[q, m], 0.0)
        shifted[q] = total
    for kk in range(4):
        for ll in range(4):
            block = jnp.zeros((128, 128), F32)
            for q in range(4):
                same = (e * 0 + pairing[kk, q]) == ll
                block = block + jnp.where(same, shifted[q], 0.0)
            hi, lo = split(block)
            row = pl.ds(128 * ((kk % 2) * 2 + kk // 2), 128)
            col = 128 * ((ll % 2) * 2 + ll // 2)
            kmat[row, pl.ds(col, 128)] = hi
            kmat[row, pl.ds(512 + col, 128)] = hi
            kmat[row, pl.ds(1024 + col, 128)] = lo

    def plane_forward(k, ts, slot):
        def in_plane(i, carry):
            p, device = plane(me, i)
            send(zb.at[k, ts, :, pl.ds(3 * p, 3)], pb.at[k, ts, :, mine], ps.at[slot], pr.at[slot], device)
            return carry

        lax.fori_loop(1, 32, in_plane, 0)
        pltpu.make_async_copy(zb.at[k, ts, :, mine], pb.at[k, ts, :, mine], pr.at[slot]).start()

    def plane_back(t):
        def in_plane(i, carry):
            p, device = plane(me, i)
            send(cb.at[t, :, :, pl.ds(3 * p, 3)], rb.at[t, :, :, mine], bs.at[t], br.at[t], device)
            return carry

        lax.fori_loop(1, 32, in_plane, 0)
        pltpu.make_async_copy(cb.at[t, :, :, mine], rb.at[t, :, :, mine], br.at[t]).start()

    def z_back(t):
        wait_for(rb.at[t], br.at[t])
        rows = pl.ds(pl.multiple_of(96 * me["zl"], 8), 96)
        for k in range(2):

            def along_z(d, carry, k=k):
                z, device = ring_z(me, d)
                send(rb.at[t, k, z], out.at[t, k, me["zh"], rows], ws.at[t], wr.at[t], device)
                return carry

            lax.fori_loop(1, 8, along_z, 0)
            pltpu.make_async_copy(rb.at[t, k, my_z], out.at[t, k, me["zh"], rows], wr.at[t]).start()

    def convolve(t):
        for k in range(2):
            for z in range(8):
                rows = pl.ds(256 * k + 32 * z, 32)
                for j in range(3):
                    hi, lo = split(pb[k, t, z, pl.ds(j, 32, stride=3), :])
                    cols = pl.ds(128 * j, 128)
                    xs[rows, cols] = hi
                    xs[pl.ds(512 + 256 * k + 32 * z, 32), cols] = lo
                    xs[pl.ds(1024 + 256 * k + 32 * z, 32), cols] = hi
        result = jnp.dot(kmat[...], xs[...], preferred_element_type=F32)
        for j in range(3):
            scaled = result[:, 128 * j : 128 * (j + 1)] * coupling[pl.ds(j, 1), pl.ds(128 * t, 128)]
            for k in range(2):
                for z in range(8):
                    start = 256 * k + 32 * z
                    cb[t, k, z, pl.ds(j, 32, stride=3), :] = scaled[start : start + 32, :]

    for t in range(T):
        wait_for(zb.at[0, t], zr.at[0, t])
    plane_forward(0, pl.ds(0, T), 0)
    for t in range(T):
        wait_for(zb.at[1, t], zr.at[1, t])
        plane_forward(1, pl.ds(t, 1), 1 + t)
        if t == 0:
            wait_for(pb.at[0], pr.at[0])
        if t == 2:
            z_back(0)
        wait_for(pb.at[1, t], pr.at[1 + t])
        convolve(t)
        plane_back(t)
    z_back(1)
    z_back(2)

    for t in range(T):
        wait_for(out.at[t], wr.at[t])
    for k in range(2):
        for t in range(T):
            wait_for(zb.at[k, t, pl.ds(0, 7)], zs.at[k, t])
    wait_for(pb.at[0, :, :, pl.ds(0, 93)], ps.at[0])
    for t in range(T):
        wait_for(pb.at[1, pl.ds(t, 1), :, pl.ds(0, 93)], ps.at[1 + t])
        wait_for(rb.at[t, :, :, pl.ds(0, 93)], bs.at[t])
        wait_for(rb.at[t, :, pl.ds(0, 7)], ws.at[t])


def exchange(lin, weight, shift, pairing, coupling):
    dma = pltpu.SemaphoreType.DMA
    return pl.pallas_call(
        exchange_kernel,
        out_shape=jax.ShapeDtypeStruct((T, 2, 2, B, 128), F32),
        in_specs=[VMEM, SMEM, SMEM, SMEM, VMEM],
        out_specs=VMEM,
        scratch_shapes=[
            pltpu.VMEM((2, T, 8, 96, 128), F32),
            pltpu.VMEM((2, T, 8, 96, 128), F32),
            pltpu.VMEM((T, 2, 8, 96, 128), F32),
            pltpu.VMEM((T, 2, 8, 96, 128), F32),
            pltpu.VMEM((512, 1536), BF16),
            pltpu.VMEM((4, 128, 128), F32),
            pltpu.VMEM((1536, 384), BF16),
            dma((2, T)), dma((2, T)),
            dma((4,)), dma((4,)),
            dma((T,)), dma((T,)),
            dma((T,)), dma((T,)),
        ],
        compiler_params=pltpu.CompilerParams(
            collective_id=1, has_side_effects=True, vmem_limit_bytes=48 << 20
        ),
        name="exchange",
    )(lin, weight, shift, pairing, coupling)


def force_kernel(g_ref, s_ref, w_ref, sigma_ref, f_ref, left, right):
    for n in range(4):
        part, k = n // 2, n % 2
        hi, lo = split(g_ref[part, 0, k])
        for base, value in ((0, hi), (4 * B, hi), (8 * B, lo)):
            left[:, pl.ds(base + n * B, B)] = value
        for t in range(T):
            s = s_ref[t, k, part]
            sigma_ref[part, 0, k, :, pl.ds(128 * t, 128)] = s
            hi, lo = split(s if part == 0 else -s)
            for base, value in ((0, hi), (4 * B, lo), (8 * B, hi)):
                right[pl.ds(base + n * B, B), pl.ds(128 * t, 128)] = value
    total = jnp.dot(left[...], right[...], preferred_element_type=F32) * w_ref[0]
    for t in range(T):
        f_ref[t] = total[:, 128 * t : 128 * (t + 1)]


def sigma_and_force(green, raw, energy_weight):
    return pl.pallas_call(
        force_kernel,
        out_shape=(
            jax.ShapeDtypeStruct((2, 1, 2, B, B), F32),
            jax.ShapeDtypeStruct((T, B, 128), F32),
        ),
        in_specs=[VMEM, VMEM, SMEM],
        out_specs=(VMEM, VMEM),
        scratch_shapes=[
            pltpu.VMEM((B, 12 * B), BF16),
            pltpu.VMEM((12 * B, B), BF16),
        ],
        compiler_params=pltpu.CompilerParams(vmem_limit_bytes=48 << 20),
        name="sigma_force",
    )(green, raw, energy_weight)


def reduce_kernel(f, fw, out, near, own, far, ns, nr, fs, fr):
    me = here()
    my_z = me["zh"] * 4 + me["zl"]
    my_p = (me["x"] * 4 + me["y"]) * 2 + me["c"]
    greet(me)

    def in_plane(i, carry):
        p, device = plane(me, i)
        send(f.at[:, :, pl.ds(3 * p, 3)], near.at[my_p], ns, nr, device)
        return carry

    lax.fori_loop(1, 32, in_plane, 0)
    pltpu.make_async_copy(f.at[:, :, pl.ds(3 * my_p, 3)], near.at[my_p], nr).start()
    wait_for(near, nr)
    total = near[0]
    for p in range(1, 32):
        total = total + near[p]
    own[...] = total

    def along_z(d, carry):
        z, device = ring_z(me, d)
        send(own.at[:, lax.rem(z, 4)], far.at[my_z], fs, fr, device)
        return carry

    lax.fori_loop(1, 8, along_z, 0)
    pltpu.make_async_copy(own.at[:, me["zl"]], far.at[my_z], fr).start()
    wait_for(far, fr)
    total = far[0]
    for z in range(1, 8):
        total = total + far[z]
    for t in range(T):
        out[:, pl.ds(128 * t, 128)] = total[t] * fw[:, pl.ds(128 * t, 128)]
    wait_for(near.at[pl.ds(0, 31)], ns)
    wait_for(far.at[pl.ds(0, 7)], fs)


def reduce_force(partial, force_weight):
    dma = pltpu.SemaphoreType.DMA
    return pl.pallas_call(
        reduce_kernel,
        out_shape=jax.ShapeDtypeStruct((3, B), F32),
        in_specs=[VMEM, VMEM],
        out_specs=VMEM,
        scratch_shapes=[
            pltpu.VMEM((32, T, 4, 3, 128), F32),
            pltpu.VMEM((T, 4, 3, 128), F32),
            pltpu.VMEM((8, T, 3, 128), F32),
            dma, dma, dma, dma,
        ],
        compiler_params=pltpu.CompilerParams(collective_id=2, has_side_effects=True),
        name="reduce_force",
    )(partial.reshape(T, 4, 96, 128), force_weight)


def per_device(
    system_matrix, approx_inverse, mode_weight, phonon_shift, pairing, coupling, energy_weight, force_weight
):
    green, lin = newton(system_matrix, approx_inverse.reshape(2, 2, B))
    raw = exchange(lin, mode_weight, phonon_shift, pairing, coupling)
    sigma, partial = sigma_and_force(green, raw, energy_weight)
    force = reduce_force(partial, force_weight)
    return green, sigma, force


def solution(mesh):
    torus = Mesh(mesh.devices.reshape(4, 4, 4, 2, 2), AXES)
    return jax.shard_map(
        per_device,
        mesh=torus,
        in_specs=(
            P(None, ENERGY, "zh", None, None),
            P(None, ENERGY, "zh", None),
            P(),
            P(),
            P(),
            P(ENERGY, None),
            P(ENERGY),
            P(ENERGY, None),
        ),
        out_specs=(
            P(None, ENERGY, "zh", None, None),
            P(None, ENERGY, "zh", None, None),
            P(ENERGY, None),
        ),
        check_vma=False,
    )
```

```python
import functools

import jax
import jax.numpy as jnp
from jax import lax
from jax.experimental import pallas as pl
from jax.experimental.pallas import tpu as pltpu
from jax.sharding import Mesh
from jax.sharding import PartitionSpec as P

AXES = ("zl", "x", "y", "c", "zh")
ENERGY = ("zl", "x", "y", "c")
MESH_ID = pl.DeviceIdType.MESH
F32 = jnp.float32
BF16 = jnp.bfloat16
B = 384
T = 3
VMEM = pl.BlockSpec(memory_space=pltpu.VMEM)
SMEM = pl.BlockSpec(memory_space=pltpu.SMEM)


def split(x):
    hi = x.astype(BF16)
    lo = (x - hi.astype(F32)).astype(BF16)
    return hi, lo


def put_left(ref, real, imag, row):
    rows = pl.ds(row, B)
    for col, part in ((0, real), (B, imag)):
        hi, lo = split(part)
        ref[rows, pl.ds(col, B)] = hi
        ref[rows, pl.ds(2 * B + col, B)] = hi
        ref[rows, pl.ds(4 * B + col, B)] = lo


def put_right(ref, real, imag):
    rh, rl = split(real)
    ih, il = split(imag)
    for base, r, i in ((0, rh, ih), (2 * B, rl, il), (4 * B, rh, ih)):
        for t in range(T):
            cut = slice(128 * t, 128 * (t + 1))
            ref[pl.ds(base, B), pl.ds(256 * t, 128)] = r[:, cut]
            ref[pl.ds(base, B), pl.ds(256 * t + 128, 128)] = i[:, cut]
            ref[pl.ds(base + B, B), pl.ds(256 * t, 128)] = -i[:, cut]
            ref[pl.ds(base + B, B), pl.ds(256 * t + 128, 128)] = r[:, cut]


def parts_of(wide):
    real = jnp.concatenate([wide[:, 256 * t : 256 * t + 128] for t in range(T)], axis=1)
    imag = jnp.concatenate([wide[:, 256 * t + 128 : 256 * t + 256] for t in range(T)], axis=1)
    return real, imag


def newton_but_last(k, matrix, approx, left, right, xr, xi):
    row = lax.broadcasted_iota(jnp.int32, (B, B), 0)
    col = lax.broadcasted_iota(jnp.int32, (B, B), 1)
    eye = row == col
    one = jnp.where(eye, 1.0, 0.0).astype(F32)
    cr = approx[0, pl.ds(k, 1), :]
    ci = approx[1, pl.ds(k, 1), :]
    cr_col = jnp.sum(jnp.where(eye, cr, 0.0), axis=1, keepdims=True)
    ci_col = jnp.sum(jnp.where(eye, ci, 0.0), axis=1, keepdims=True)
    mr = matrix[k, 0]
    mi = matrix[k, 1]
    yr = one - (mr * cr - mi * ci)
    yi = -(mr * ci + mi * cr)
    put_left(left, yr, yi, 0)
    put_right(right, yr, yi)
    ar = one + yr
    xr[...] = cr_col * ar - ci_col * yi
    xi[...] = cr_col * yi + ci_col * ar
    y0 = jnp.dot(left[pl.ds(0, B), :], right[...], preferred_element_type=F32)
    y0r, y0i = parts_of(y0)
    put_left(left, y0r, y0i, B)
    put_left(left, xr[...], xi[...], 0)
    put_right(right, y0r, y0i)
    both = jnp.dot(left[...], right[...], preferred_element_type=F32)
    dr, di = parts_of(both[:B])
    y1r, y1i = parts_of(both[B:])
    x1r = xr[...] + dr
    x1i = xi[...] + di
    xr[...] = x1r
    xi[...] = x1i
    put_left(left, x1r, x1i, 0)
    put_right(right, y1r, y1i)


def newton_last(k, t, left, right, xr, xi, lin):
    last = jnp.dot(left[pl.ds(0, B), :], right[:, pl.ds(256 * t, 256)], preferred_element_type=F32)
    cols = pl.ds(128 * t, 128)
    lin[k, t, 0] = xr[:, cols] + last[:, :128]
    lin[k, t, 1] = xi[:, cols] + last[:, 128:]


def here():
    return {a: lax.axis_index(a) for a in AXES}


def ring_z(me, d):
    z = lax.rem(me["zh"] * 4 + me["zl"] + d, 8)
    return z, (lax.rem(z, 4), me["x"], me["y"], me["c"], z // 4)


def plane(me, i):
    x = lax.rem(me["x"] + i // 8, 4)
    y = lax.rem(me["y"] + lax.rem(i // 2, 4), 4)
    c = lax.rem(me["c"] + lax.rem(i, 2), 2)
    return (x * 4 + y) * 2 + c, (me["zl"], x, y, c, me["zh"])


def greet(me):
    barrier = pltpu.get_barrier_semaphore()

    def along_z(d, carry):
        pl.semaphore_signal(barrier, inc=1, device_id=ring_z(me, d)[1], device_id_type=MESH_ID)
        return carry

    def in_plane(i, carry):
        pl.semaphore_signal(barrier, inc=1, device_id=plane(me, i)[1], device_id_type=MESH_ID)
        return carry

    lax.fori_loop(1, 8, along_z, 0)
    lax.fori_loop(1, 32, in_plane, 0)
    return barrier


def send(src, dst, ssem, rsem, device):
    pltpu.make_async_remote_copy(
        src_ref=src, dst_ref=dst, send_sem=ssem, recv_sem=rsem, device_id=device, device_id_type=MESH_ID
    ).start()


def wait_for(ref, sem):
    pltpu.make_async_copy(ref, ref, sem).wait()


def step_kernel(
    matrix_hbm, approx, weight, shift, pairing, coupling, energy_weight, force_weight,
    out, lin, force,
    matrix, left, right, xr, xi, zb, pb, cb, rb, kmat, shifted, xs, fleft, fright, fb, near, own, far,
    ms, zs, zr, ps, pr, bs, br, ws, wr, ns, nr, fs, fr,
):
    me = here()
    my_z = me["zh"] * 4 + me["zl"]
    my_p = (me["x"] * 4 + me["y"]) * 2 + me["c"]
    mine = pl.ds(3 * my_p, 3)
    my_rows = pl.ds(pl.multiple_of(96 * me["zl"], 8), 96)

    loads = [pltpu.make_async_copy(matrix_hbm.at[:, 0, k], matrix.at[k], ms.at[k]) for k in range(2)]
    for load in loads:
        load.start()
    barrier = greet(me)

    def z_forward(k, t):
        def along_z(d, carry):
            z, device = ring_z(me, d)
            rows = pl.ds(pl.multiple_of(96 * lax.rem(z, 4), 8), 96)
            send(lin.at[k, t, z // 4, rows], zb.at[k, t, my_z], zs.at[k, t], zr.at[k, t], device)
            return carry

        lax.fori_loop(1, 8, along_z, 0)
        pltpu.make_async_copy(lin.at[k, t, me["zh"], my_rows], zb.at[k, t, my_z], zr.at[k, t]).start()

    def plane_forward(k, t):
        wait_for(zb.at[k, t], zr.at[k, t])

        def in_plane(i, carry):
            p, device = plane(me, i)
            send(zb.at[k, t, :, pl.ds(3 * p, 3)], pb.at[k, t, :, mine], ps.at[k, t], pr.at[k, t], device)
            return carry

        lax.fori_loop(1, 32, in_plane, 0)
        pltpu.make_async_copy(zb.at[k, t, :, mine], pb.at[k, t, :, mine], pr.at[k, t]).start()

    def plane_back(k, t):
        def in_plane(i, carry):
            p, device = plane(me, i)
            send(cb.at[t, k, :, pl.ds(3 * p, 3)], rb.at[t, k, :, mine], bs.at[t, k], br.at[t, k], device)
            return carry

        lax.fori_loop(1, 32, in_plane, 0)
        pltpu.make_async_copy(cb.at[t, k, :, mine], rb.at[t, k, :, mine], br.at[t, k]).start()

    def z_back(k, t):
        wait_for(rb.at[t, k], br.at[t, k])

        def along_z(d, carry):
            z, device = ring_z(me, d)
            send(rb.at[t, k, z], out.at[t, k, me["zh"], my_rows], ws.at[t, k], wr.at[t, k], device)
            return carry

        lax.fori_loop(1, 8, along_z, 0)
        pltpu.make_async_copy(rb.at[t, k, my_z], out.at[t, k, me["zh"], my_rows], wr.at[t, k]).start()

    def build_kernel():
        e = lax.broadcasted_iota(jnp.int32, (128, 128), 0)
        f = lax.broadcasted_iota(jnp.int32, (128, 128), 1)
        for q in range(4):
            total = jnp.zeros((128, 128), F32)
            for m in range(6):
                total = total + jnp.where(f == e - shift[q, m], weight[q, m], 0.0)
            shifted[q] = total
        for kk in range(4):
            for ll in range(4):
                block = jnp.zeros((128, 128), F32)
                for q in range(4):
                    same = (e * 0 + pairing[kk, q]) == ll
                    block = block + jnp.where(same, shifted[q], 0.0)
                hi, lo = split(block)
                row = pl.ds(128 * ((kk % 2) * 2 + kk // 2), 128)
                col = 128 * ((ll % 2) * 2 + ll // 2)
                kmat[row, pl.ds(col, 128)] = hi
                kmat[row, pl.ds(512 + col, 128)] = hi
                kmat[row, pl.ds(1024 + col, 128)] = lo

    def convolve(t):
        for k in range(2):
            wait_for(pb.at[k, t], pr.at[k, t])
            for z in range(8):
                rows = pl.ds(256 * k + 32 * z, 32)
                for j in range(3):
                    hi, lo = split(pb[k, t, z, pl.ds(j, 32, stride=3), :])
                    cols = pl.ds(128 * j, 128)
                    xs[rows, cols] = hi
                    xs[pl.ds(512 + 256 * k + 32 * z, 32), cols] = lo
                    xs[pl.ds(1024 + 256 * k + 32 * z, 32), cols] = hi
        for k in range(2):
            result = jnp.dot(kmat[pl.ds(256 * k, 256), :], xs[...], preferred_element_type=F32)
            for j in range(3):
                scaled = result[:, 128 * j : 128 * (j + 1)] * coupling[pl.ds(j, 1), pl.ds(128 * t, 128)]
                for z in range(8):
                    cb[t, k, z, pl.ds(j, 32, stride=3), :] = scaled[32 * z : 32 * z + 32, :]
            plane_back(k, t)

    def build_force_left():
        for n in range(4):
            part, k = n // 2, n % 2
            for t in range(T):
                hi, lo = split(lin[k, t, part])
                for base, value in ((0, hi), (4 * B, hi), (8 * B, lo)):
                    fleft[:, pl.ds(base + n * B + 128 * t, 128)] = value

    def force_part(t):
        for k in range(2):
            wait_for(out.at[t, k], wr.at[t, k])
            for part in range(2):
                s = out[t, k, part]
                n = 2 * part + k
                hi, lo = split(s if part == 0 else -s)
                for base, value in ((0, hi), (4 * B, lo), (8 * B, hi)):
                    fright[pl.ds(base + n * B, B), :] = value
        total = jnp.dot(fleft[...], fright[...], preferred_element_type=F32) * energy_weight[0]
        for z in range(4):
            fb[t, z] = total[96 * z : 96 * (z + 1), :]

        def in_plane(i, carry):
            p, device = plane(me, i)
            send(fb.at[t, :, pl.ds(3 * p, 3)], near.at[t, my_p], ns.at[t], nr.at[t], device)
            return carry

        lax.fori_loop(1, 32, in_plane, 0)
        pltpu.make_async_copy(fb.at[t, :, mine], near.at[t, my_p], nr.at[t]).start()

    def force_along_z(t):
        wait_for(near.at[t], nr.at[t])
        total = near[t, 0]
        for p in range(1, 32):
            total = total + near[t, p]
        own[t] = total

        def along_z(d, carry):
            z, device = ring_z(me, d)
            send(own.at[t, lax.rem(z, 4)], far.at[t, my_z], fs.at[t], fr.at[t], device)
            return carry

        lax.fori_loop(1, 8, along_z, 0)
        pltpu.make_async_copy(own.at[t, me["zl"]], far.at[t, my_z], fr.at[t]).start()

    def force_out(t):
        wait_for(far.at[t], fr.at[t])
        total = far[t, 0]
        for z in range(1, 8):
            total = total + far[t, z]
        cols = pl.ds(128 * t, 128)
        force[:, cols] = total * force_weight[:, cols]

    loads[0].wait()
    newton_but_last(0, matrix, approx, left, right, xr, xi)
    pl.semaphore_wait(barrier, 38)
    for t in range(T):
        newton_last(0, t, left, right, xr, xi, lin)
        if t < 2:
            z_forward(0, t)
    loads[1].wait()
    newton_but_last(1, matrix, approx, left, right, xr, xi)
    for t in range(T):
        newton_last(1, t, left, right, xr, xi, lin)
        if t < 2:
            z_forward(1, t)
    z_forward(0, 2)
    z_forward(1, 2)
    plane_forward(0, 0)
    build_kernel()
    plane_forward(0, 1)
    plane_forward(1, 0)
    convolve(0)
    plane_forward(1, 1)
    convolve(1)
    plane_forward(0, 2)
    z_back(0, 0)
    z_back(1, 0)
    build_force_left()
    plane_forward(1, 2)
    z_back(0, 1)
    z_back(1, 1)
    convolve(2)
    z_back(0, 2)
    z_back(1, 2)
    force_part(0)
    force_part(1)
    force_along_z(0)
    force_along_z(1)
    force_part(2)
    force_along_z(2)
    for t in range(T):
        force_out(t)

    for t in range(T):
        for k in range(2):
            wait_for(zb.at[k, t, pl.ds(0, 7)], zs.at[k, t])
            wait_for(pb.at[k, t, :, pl.ds(0, 93)], ps.at[k, t])
            wait_for(rb.at[t, k, :, pl.ds(0, 93)], bs.at[t, k])
            wait_for(rb.at[t, k, pl.ds(0, 7)], ws.at[t, k])
        wait_for(near.at[t, pl.ds(0, 31)], ns.at[t])
        wait_for(far.at[t, pl.ds(0, 7)], fs.at[t])


def step(matrix, approx, weight, shift, pairing, coupling, energy_weight, force_weight):
    dma = pltpu.SemaphoreType.DMA
    return pl.pallas_call(
        step_kernel,
        out_shape=(
            jax.ShapeDtypeStruct((T, 2, 2, B, 128), F32),
            jax.ShapeDtypeStruct((2, T, 2, B, 128), F32),
            jax.ShapeDtypeStruct((3, B), F32),
        ),
        in_specs=[pl.BlockSpec(memory_space=pl.ANY), VMEM, SMEM, SMEM, SMEM, VMEM, SMEM, VMEM],
        out_specs=(VMEM, VMEM, VMEM),
        scratch_shapes=[
            pltpu.VMEM((2, 2, B, B), F32),
            pltpu.VMEM((2 * B, 6 * B), BF16),
            pltpu.VMEM((6 * B, 2 * B), BF16),
            pltpu.VMEM((B, B), F32),
            pltpu.VMEM((B, B), F32),
            pltpu.VMEM((2, T, 8, 96, 128), F32),
            pltpu.VMEM((2, T, 8, 96, 128), F32),
            pltpu.VMEM((T, 2, 8, 96, 128), F32),
            pltpu.VMEM((T, 2, 8, 96, 128), F32),
            pltpu.VMEM((512, 1536), BF16),
            pltpu.VMEM((4, 128, 128), F32),
            pltpu.VMEM((1536, 384), BF16),
            pltpu.VMEM((B, 12 * B), BF16),
            pltpu.VMEM((12 * B, 128), BF16),
            pltpu.VMEM((T, 4, 96, 128), F32),
            pltpu.VMEM((T, 32, 4, 3, 128), F32),
            pltpu.VMEM((T, 4, 3, 128), F32),
            pltpu.VMEM((T, 8, 3, 128), F32),
            dma((2,)),
            dma((2, T)), dma((2, T)),
            dma((2, T)), dma((2, T)),
            dma((T, 2)), dma((T, 2)),
            dma((T, 2)), dma((T, 2)),
            dma((T,)), dma((T,)),
            dma((T,)), dma((T,)),
        ],
        compiler_params=pltpu.CompilerParams(
            collective_id=1, has_side_effects=True, vmem_limit_bytes=52 << 20
        ),
        name="step",
    )(matrix, approx, weight, shift, pairing, coupling, energy_weight, force_weight)


def layout_kernel(raw, lin, f_in, green, sigma, f_out):
    part = pl.program_id(0)
    k = pl.program_id(1)
    for t in range(T):
        cols = pl.ds(128 * t, 128)
        green[0, 0, 0, :, cols] = lin[k, t, part]
        sigma[0, 0, 0, :, cols] = raw[t, k, part]
    f_out[...] = f_in[...]


def final_layouts(raw, lin, force):
    block = pl.BlockSpec((1, 1, 1, B, B), lambda part, k: (part, 0, k, 0, 0))
    return pl.pallas_call(
        layout_kernel,
        grid=(2, 2),
        out_shape=(
            jax.ShapeDtypeStruct((2, 1, 2, B, B), F32),
            jax.ShapeDtypeStruct((2, 1, 2, B, B), F32),
            jax.ShapeDtypeStruct((3, B), F32),
        ),
        in_specs=[VMEM, VMEM, VMEM],
        out_specs=(block, block, pl.BlockSpec((3, B), lambda part, k: (0, 0))),
        name="layouts",
    )(raw, lin, force)


def per_device(
    system_matrix, approx_inverse, mode_weight, phonon_shift, pairing, coupling, energy_weight, force_weight
):
    raw, lin, force = step(
        system_matrix, approx_inverse.reshape(2, 2, B), mode_weight, phonon_shift, pairing, coupling,
        energy_weight, force_weight,
    )
    return final_layouts(raw, lin, force)


def solution(mesh):
    torus = Mesh(mesh.devices.reshape(4, 4, 4, 2, 2), AXES)
    return jax.shard_map(
        per_device,
        mesh=torus,
        in_specs=(
            P(None, ENERGY, "zh", None, None),
            P(None, ENERGY, "zh", None),
            P(),
            P(),
            P(),
            P(ENERGY, None),
            P(ENERGY),
            P(ENERGY, None),
        ),
        out_specs=(
            P(None, ENERGY, "zh", None, None),
            P(None, ENERGY, "zh", None, None),
            P(ENERGY, None),
        ),
        check_vma=False,
    )
```

```python
import functools

import jax
import jax.numpy as jnp
from jax import lax
from jax.experimental import pallas as pl
from jax.experimental.pallas import tpu as pltpu
from jax.sharding import Mesh
from jax.sharding import PartitionSpec as P

AXES = ("zl", "x", "y", "c", "zh")
ENERGY = ("zl", "x", "y", "c")
MESH_ID = pl.DeviceIdType.MESH
F32 = jnp.float32
BF16 = jnp.bfloat16
B = 384
T = 3
VMEM = pl.BlockSpec(memory_space=pltpu.VMEM)
SMEM = pl.BlockSpec(memory_space=pltpu.SMEM)


def split(x):
    hi = x.astype(BF16)
    lo = (x - hi.astype(F32)).astype(BF16)
    return hi, lo


def put_left(ref, real, imag, row):
    rows = pl.ds(row, B)
    for col, part in ((0, real), (B, imag)):
        hi, lo = split(part)
        ref[rows, pl.ds(col, B)] = hi
        ref[rows, pl.ds(2 * B + col, B)] = hi
        ref[rows, pl.ds(4 * B + col, B)] = lo


def put_right(ref, real, imag):
    rh, rl = split(real)
    ih, il = split(imag)
    for base, r, i in ((0, rh, ih), (2 * B, rl, il), (4 * B, rh, ih)):
        for t in range(T):
            cut = slice(128 * t, 128 * (t + 1))
            ref[pl.ds(base, B), pl.ds(256 * t, 128)] = r[:, cut]
            ref[pl.ds(base, B), pl.ds(256 * t + 128, 128)] = i[:, cut]
            ref[pl.ds(base + B, B), pl.ds(256 * t, 128)] = -i[:, cut]
            ref[pl.ds(base + B, B), pl.ds(256 * t + 128, 128)] = r[:, cut]


def parts_of(wide):
    real = jnp.concatenate([wide[:, 256 * t : 256 * t + 128] for t in range(T)], axis=1)
    imag = jnp.concatenate([wide[:, 256 * t + 128 : 256 * t + 256] for t in range(T)], axis=1)
    return real, imag


def newton_but_last(k, matrix, approx, left, right, xr, xi):
    row = lax.broadcasted_iota(jnp.int32, (B, B), 0)
    col = lax.broadcasted_iota(jnp.int32, (B, B), 1)
    eye = row == col
    one = jnp.where(eye, 1.0, 0.0).astype(F32)
    cr = approx[0, pl.ds(k, 1), :]
    ci = approx[1, pl.ds(k, 1), :]
    cr_col = jnp.sum(jnp.where(eye, cr, 0.0), axis=1, keepdims=True)
    ci_col = jnp.sum(jnp.where(eye, ci, 0.0), axis=1, keepdims=True)
    mr = matrix[k, 0]
    mi = matrix[k, 1]
    yr = one - (mr * cr - mi * ci)
    yi = -(mr * ci + mi * cr)
    put_left(left, yr, yi, 0)
    put_right(right, yr, yi)
    ar = one + yr
    xr[...] = cr_col * ar - ci_col * yi
    xi[...] = cr_col * yi + ci_col * ar
    y0 = jnp.dot(left[pl.ds(0, B), :], right[...], preferred_element_type=F32)
    y0r, y0i = parts_of(y0)
    put_left(left, y0r, y0i, B)
    put_left(left, xr[...], xi[...], 0)
    put_right(right, y0r, y0i)
    both = jnp.dot(left[...], right[...], preferred_element_type=F32)
    dr, di = parts_of(both[:B])
    y1r, y1i = parts_of(both[B:])
    x1r = xr[...] + dr
    x1i = xi[...] + di
    xr[...] = x1r
    xi[...] = x1i
    put_left(left, x1r, x1i, 0)
    put_right(right, y1r, y1i)


def newton_last(k, t, left, right, xr, xi, lin):
    last = jnp.dot(left[pl.ds(0, B), :], right[:, pl.ds(256 * t, 256)], preferred_element_type=F32)
    cols = pl.ds(128 * t, 128)
    lin[k, t, 0] = xr[:, cols] + last[:, :128]
    lin[k, t, 1] = xi[:, cols] + last[:, 128:]


def here():
    return {a: lax.axis_index(a) for a in AXES}


def ring_z(me, d):
    z = lax.rem(me["zh"] * 4 + me["zl"] + d, 8)
    return z, (lax.rem(z, 4), me["x"], me["y"], me["c"], z // 4)


def plane(me, i):
    x = lax.rem(me["x"] + i // 8, 4)
    y = lax.rem(me["y"] + lax.rem(i // 2, 4), 4)
    c = lax.rem(me["c"] + lax.rem(i, 2), 2)
    return (x * 4 + y) * 2 + c, (me["zl"], x, y, c, me["zh"])


def greet(me):
    barrier = pltpu.get_barrier_semaphore()

    def along_z(d, carry):
        pl.semaphore_signal(barrier, inc=1, device_id=ring_z(me, d)[1], device_id_type=MESH_ID)
        return carry

    def in_plane(i, carry):
        pl.semaphore_signal(barrier, inc=1, device_id=plane(me, i)[1], device_id_type=MESH_ID)
        return carry

    lax.fori_loop(1, 8, along_z, 0)
    lax.fori_loop(1, 32, in_plane, 0)
    return barrier


def send(src, dst, ssem, rsem, device):
    pltpu.make_async_remote_copy(
        src_ref=src, dst_ref=dst, send_sem=ssem, recv_sem=rsem, device_id=device, device_id_type=MESH_ID
    ).start()


def wait_for(ref, sem):
    pltpu.make_async_copy(ref, ref, sem).wait()


def step_kernel(
    matrix_hbm, approx_hbm, weight_hbm, shift_hbm, pairing_hbm, coupling_hbm, energy_hbm, force_hbm,
    green_hbm, sigma_hbm, force,
    approx, weight, shift, pairing, coupling, energy_weight, force_weight, small_sem, lin, out,
    matrix, left, right, xr, xi, zb, pb, cb, rb, kmat, shifted, xs, fleft, fright, fa, fb, near, own, far,
    ms, zs, zr, ps, pr, bs, br, ws, wr, ns, nr, fs, fr, gs, ss,
):
    me = here()
    my_z = me["zh"] * 4 + me["zl"]
    my_p = (me["x"] * 4 + me["y"]) * 2 + me["c"]
    mine = pl.ds(3 * my_p, 3)
    my_rows = pl.ds(pl.multiple_of(96 * me["zl"], 8), 96)

    loads = [pltpu.make_async_copy(matrix_hbm.at[:, 0, k], matrix.at[k], ms.at[k]) for k in range(2)]
    small = [
        pltpu.make_async_copy(src, dst, small_sem.at[n])
        for n, (src, dst) in enumerate(
            (
                (approx_hbm, approx),
                (weight_hbm, weight),
                (shift_hbm, shift),
                (pairing_hbm, pairing),
                (coupling_hbm, coupling),
                (energy_hbm, energy_weight),
                (force_hbm, force_weight),
            )
        )
    ]
    for load in small + loads:
        load.start()
    barrier = greet(me)

    def green_out(k, t, part):
        place = green_hbm.at[part, 0, k, :, pl.ds(128 * t, 128)]
        return pltpu.make_async_copy(lin.at[k, t, part], place, gs.at[k, t, part])

    def sigma_out(k, t, part):
        place = sigma_hbm.at[part, 0, k, :, pl.ds(128 * t, 128)]
        return pltpu.make_async_copy(out.at[t, k, part], place, ss.at[k, t, part])

    def z_forward(k, t):
        def along_z(d, carry):
            z, device = ring_z(me, d)
            rows = pl.ds(pl.multiple_of(96 * lax.rem(z, 4), 8), 96)
            send(lin.at[k, t, z // 4, rows], zb.at[k, t, my_z], zs.at[k, t], zr.at[k, t], device)
            return carry

        lax.fori_loop(1, 8, along_z, 0)
        pltpu.make_async_copy(lin.at[k, t, me["zh"], my_rows], zb.at[k, t, my_z], zr.at[k, t]).start()

    def plane_forward(k, t):
        wait_for(zb.at[k, t], zr.at[k, t])

        def in_plane(i, carry):
            p, device = plane(me, i)
            send(zb.at[k, t, :, pl.ds(3 * p, 3)], pb.at[k, t, :, mine], ps.at[k, t], pr.at[k, t], device)
            return carry

        lax.fori_loop(1, 32, in_plane, 0)
        pltpu.make_async_copy(zb.at[k, t, :, mine], pb.at[k, t, :, mine], pr.at[k, t]).start()

    def plane_back(k, t):
        def in_plane(i, carry):
            p, device = plane(me, i)
            send(cb.at[t, k, :, pl.ds(3 * p, 3)], rb.at[t, k, :, mine], bs.at[t, k], br.at[t, k], device)
            return carry

        lax.fori_loop(1, 32, in_plane, 0)
        pltpu.make_async_copy(cb.at[t, k, :, mine], rb.at[t, k, :, mine], br.at[t, k]).start()

    def z_back(k, t):
        wait_for(rb.at[t, k], br.at[t, k])

        def along_z(d, carry):
            z, device = ring_z(me, d)
            send(rb.at[t, k, z], out.at[t, k, me["zh"], my_rows], ws.at[t, k], wr.at[t, k], device)
            return carry

        lax.fori_loop(1, 8, along_z, 0)
        pltpu.make_async_copy(rb.at[t, k, my_z], out.at[t, k, me["zh"], my_rows], wr.at[t, k]).start()

    def build_kernel():
        e = lax.broadcasted_iota(jnp.int32, (128, 128), 0)
        f = lax.broadcasted_iota(jnp.int32, (128, 128), 1)
        for q in range(4):
            total = jnp.zeros((128, 128), F32)
            for m in range(6):
                total = total + jnp.where(f == e - shift[q, m], weight[q, m], 0.0)
            shifted[q] = total
        for kk in range(4):
            for ll in range(4):
                block = jnp.zeros((128, 128), F32)
                for q in range(4):
                    same = (e * 0 + pairing[kk, q]) == ll
                    block = block + jnp.where(same, shifted[q], 0.0)
                hi, lo = split(block)
                row = pl.ds(128 * ((kk % 2) * 2 + kk // 2), 128)
                col = 128 * ((ll % 2) * 2 + ll // 2)
                kmat[row, pl.ds(col, 128)] = hi
                kmat[row, pl.ds(512 + col, 128)] = hi
                kmat[row, pl.ds(1024 + col, 128)] = lo

    def convolve(t):
        for k in range(2):
            wait_for(pb.at[k, t], pr.at[k, t])
            for z in range(8):
                rows = pl.ds(256 * k + 32 * z, 32)
                for j in range(3):
                    hi, lo = split(pb[k, t, z, pl.ds(j, 32, stride=3), :])
                    cols = pl.ds(128 * j, 128)
                    xs[rows, cols] = hi
                    xs[pl.ds(512 + 256 * k + 32 * z, 32), cols] = lo
                    xs[pl.ds(1024 + 256 * k + 32 * z, 32), cols] = hi
        for k in range(2):
            result = jnp.dot(kmat[pl.ds(256 * k, 256), :], xs[...], preferred_element_type=F32)
            for j in range(3):
                scaled = result[:, 128 * j : 128 * (j + 1)] * coupling[pl.ds(j, 1), pl.ds(128 * t, 128)]
                for z in range(8):
                    cb[t, k, z, pl.ds(j, 32, stride=3), :] = scaled[32 * z : 32 * z + 32, :]
            plane_back(k, t)

    def build_force_left():
        for k in range(2):
            for part in range(2):
                for t in range(T):
                    hi, lo = split(lin[k, t, part])
                    for term, value in ((0, hi), (1, hi), (2, lo)):
                        fleft[k, :, pl.ds((2 * term + part) * B + 128 * t, 128)] = value

    def force_term(t, k):
        wait_for(out.at[t, k], wr.at[t, k])
        for part in range(2):
            sigma_out(k, t, part).start()
            s = out[t, k, part]
            hi, lo = split(s if part == 0 else -s)
            for term, value in ((0, hi), (1, lo), (2, hi)):
                fright[pl.ds((2 * term + part) * B, B), :] = value
        return jnp.dot(fleft[k], fright[...], preferred_element_type=F32)

    def force_part(t):
        fa[...] = force_term(t, 0)
        fa[...] = (fa[...] + force_term(t, 1)) * energy_weight[0]
        for z in range(4):
            for j in range(3):
                fb[t, pl.ds(3 * z + j, 32, stride=12), :] = fa[pl.ds(96 * z + j, 32, stride=3), :]

        def in_plane(i, carry):
            p, device = plane(me, i)
            send(fb.at[t, pl.ds(12 * p, 12)], near.at[t, pl.ds(12 * my_p, 12)], ns.at[t], nr.at[t], device)
            return carry

        lax.fori_loop(1, 32, in_plane, 0)
        own_rows = pl.ds(12 * my_p, 12)
        pltpu.make_async_copy(fb.at[t, own_rows], near.at[t, own_rows], nr.at[t]).start()

    def force_along_z(t):
        wait_for(near.at[t], nr.at[t])
        total = near[t, pl.ds(0, 24), :]
        for p in range(1, 16):
            total = total + near[t, pl.ds(24 * p, 24), :]
        own[t] = total[:12] + total[12:]

        def along_z(d, carry):
            z, device = ring_z(me, d)
            send(own.at[t, pl.ds(3 * lax.rem(z, 4), 3)], far.at[t, pl.ds(3 * my_z, 3)], fs.at[t], fr.at[t], device)
            return carry

        lax.fori_loop(1, 8, along_z, 0)
        own_rows = own.at[t, pl.ds(3 * me["zl"], 3)]
        pltpu.make_async_copy(own_rows, far.at[t, pl.ds(3 * my_z, 3)], fr.at[t]).start()

    def force_out(t):
        wait_for(far.at[t], fr.at[t])
        total = far[t, pl.ds(0, 3), :]
        for z in range(1, 8):
            total = total + far[t, pl.ds(3 * z, 3), :]
        cols = pl.ds(128 * t, 128)
        force[:, cols] = total * force_weight[:, cols]

    for load in small:
        load.wait()
    loads[0].wait()
    newton_but_last(0, matrix, approx, left, right, xr, xi)
    pl.semaphore_wait(barrier, 38)
    for t in range(T):
        newton_last(0, t, left, right, xr, xi, lin)
        if t < 1:
            z_forward(0, t)
    loads[1].wait()
    newton_but_last(1, matrix, approx, left, right, xr, xi)
    for t in range(T):
        newton_last(1, t, left, right, xr, xi, lin)
        z_forward(1, t)
        if t < 2:
            z_forward(0, t + 1)
    for k in range(2):
        for t in range(T):
            for part in range(2):
                green_out(k, t, part).start()
    plane_forward(0, 0)
    build_kernel()
    plane_forward(1, 0)
    convolve(0)
    plane_forward(0, 1)
    plane_forward(1, 1)
    z_back(0, 0)
    z_back(1, 0)
    convolve(1)
    build_force_left()
    plane_forward(0, 2)
    z_back(0, 1)
    z_back(1, 1)
    plane_forward(1, 2)
    convolve(2)
    z_back(0, 2)
    z_back(1, 2)
    force_part(0)
    force_part(1)
    force_along_z(0)
    force_along_z(1)
    force_part(2)
    force_along_z(2)
    for t in range(T):
        force_out(t)

    for t in range(T):
        for k in range(2):
            for part in range(2):
                green_out(k, t, part).wait()
                sigma_out(k, t, part).wait()
            wait_for(zb.at[k, t, pl.ds(0, 7)], zs.at[k, t])
            wait_for(pb.at[k, t, :, pl.ds(0, 93)], ps.at[k, t])
            wait_for(rb.at[t, k, :, pl.ds(0, 93)], bs.at[t, k])
            wait_for(rb.at[t, k, pl.ds(0, 7)], ws.at[t, k])
        wait_for(near.at[t, pl.ds(0, 372)], ns.at[t])
        wait_for(far.at[t, pl.ds(0, 21)], fs.at[t])


def step(matrix, approx, weight, shift, pairing, coupling, energy_weight, force_weight):
    dma = pltpu.SemaphoreType.DMA
    return pl.pallas_call(
        step_kernel,
        out_shape=(
            jax.ShapeDtypeStruct((2, 1, 2, B, B), F32),
            jax.ShapeDtypeStruct((2, 1, 2, B, B), F32),
            jax.ShapeDtypeStruct((3, B), F32),
        ),
        in_specs=[pl.BlockSpec(memory_space=pltpu.HBM)] * 8,
        out_specs=(pl.BlockSpec(memory_space=pltpu.HBM), pl.BlockSpec(memory_space=pltpu.HBM), VMEM),
        scratch_shapes=[
            pltpu.VMEM((2, 2, B), F32),
            pltpu.SMEM((4, 6), F32),
            pltpu.SMEM((4, 6), jnp.int32),
            pltpu.SMEM((4, 4), jnp.int32),
            pltpu.VMEM((3, B), F32),
            pltpu.SMEM((1,), F32),
            pltpu.VMEM((3, B), F32),
            dma((7,)),
            pltpu.VMEM((2, T, 2, B, 128), F32),
            pltpu.VMEM((T, 2, 2, B, 128), F32),
            pltpu.VMEM((2, 2, B, B), F32),
            pltpu.VMEM((2 * B, 6 * B), BF16),
            pltpu.VMEM((6 * B, 2 * B), BF16),
            pltpu.VMEM((B, B), F32),
            pltpu.VMEM((B, B), F32),
            pltpu.VMEM((2, T, 8, 96, 128), F32),
            pltpu.VMEM((2, T, 8, 96, 128), F32),
            pltpu.VMEM((T, 2, 8, 96, 128), F32),
            pltpu.VMEM((T, 2, 8, 96, 128), F32),
            pltpu.VMEM((512, 1536), BF16),
            pltpu.VMEM((4, 128, 128), F32),
            pltpu.VMEM((1536, 384), BF16),
            pltpu.VMEM((2, B, 6 * B), BF16),
            pltpu.VMEM((6 * B, 128), BF16),
            pltpu.VMEM((B, 128), F32),
            pltpu.VMEM((T, B, 128), F32),
            pltpu.VMEM((T, B, 128), F32),
            pltpu.VMEM((T, 12, 128), F32),
            pltpu.VMEM((T, 24, 128), F32),
            dma((2,)),
            dma((2, T)), dma((2, T)),
            dma((2, T)), dma((2, T)),
            dma((T, 2)), dma((T, 2)),
            dma((T, 2)), dma((T, 2)),
            dma((T,)), dma((T,)),
            dma((T,)), dma((T,)),
            dma((2, T, 2)), dma((2, T, 2)),
        ],
        compiler_params=pltpu.CompilerParams(
            collective_id=1, has_side_effects=True, vmem_limit_bytes=67043328
        ),
        name="step",
    )(matrix, approx, weight, shift, pairing, coupling, energy_weight, force_weight)


def copy_kernel(green, sigma, force, green_out, sigma_out, force_out, held, arrived, left):
    moves = []
    for n, (src, dst) in enumerate(((green, green_out), (sigma, sigma_out))):
        for part in range(2):
            for k in range(2):
                for h in range(CUT):
                    rows = pl.ds(h * (B // CUT), B // CUT)
                    m = len(moves)
                    place = held.at[n, part, k, rows]
                    moves.append((
                        pltpu.make_async_copy(src.at[part, 0, k, rows], place, arrived.at[m]),
                        pltpu.make_async_copy(place, dst.at[part, 0, k, rows], left.at[m]),
                    ))
    for inward, _ in moves:
        inward.start()
    force_out[...] = force[...]
    for inward, outward in moves:
        inward.wait()
        outward.start()
    for _, outward in moves:
        outward.wait()


CUT = 2


def final_copies(green, sigma, force):
    hbm = pl.BlockSpec(memory_space=pltpu.HBM)
    large = jax.ShapeDtypeStruct((2, 1, 2, B, B), F32)
    return pl.pallas_call(
        copy_kernel,
        out_shape=(large, large, jax.ShapeDtypeStruct((3, B), F32)),
        in_specs=[hbm, hbm, VMEM],
        out_specs=(hbm, hbm, VMEM),
        scratch_shapes=[
            pltpu.VMEM((2, 2, 2, B, B), F32),
            pltpu.SemaphoreType.DMA((8 * CUT,)),
            pltpu.SemaphoreType.DMA((8 * CUT,)),
        ],
        compiler_params=pltpu.CompilerParams(vmem_limit_bytes=67043328),
        name="copies",
    )(green, sigma, force)


def per_device(
    system_matrix, approx_inverse, mode_weight, phonon_shift, pairing, coupling, energy_weight, force_weight
):
    green, sigma, force = step(
        system_matrix, approx_inverse.reshape(2, 2, B), mode_weight, phonon_shift, pairing, coupling,
        energy_weight, force_weight,
    )
    return final_copies(green, sigma, force)


def solution(mesh):
    torus = Mesh(mesh.devices.reshape(4, 4, 4, 2, 2), AXES)
    return jax.shard_map(
        per_device,
        mesh=torus,
        in_specs=(
            P(None, ENERGY, "zh", None, None),
            P(None, ENERGY, "zh", None),
            P(),
            P(),
            P(),
            P(ENERGY, None),
            P(ENERGY),
            P(ENERGY, None),
        ),
        out_specs=(
            P(None, ENERGY, "zh", None, None),
            P(None, ENERGY, "zh", None, None),
            P(ENERGY, None),
        ),
        check_vma=False,
    )
```

```python
import functools

import jax
import jax.numpy as jnp
from jax import lax
from jax.experimental import pallas as pl
from jax.experimental.pallas import tpu as pltpu
from jax.sharding import Mesh
from jax.sharding import PartitionSpec as P

AXES = ("zl", "x", "y", "c", "zh")
ENERGY = ("zl", "x", "y", "c")
MESH_ID = pl.DeviceIdType.MESH
F32 = jnp.float32
BF16 = jnp.bfloat16
B = 384
T = 3
VMEM = pl.BlockSpec(memory_space=pltpu.VMEM)
SMEM = pl.BlockSpec(memory_space=pltpu.SMEM)


def split(x):
    hi = x.astype(BF16)
    lo = (x - hi.astype(F32)).astype(BF16)
    return hi, lo


def put_left(ref, real, imag, row):
    rows = pl.ds(row, B)
    for col, part in ((0, real), (B, imag)):
        hi, lo = split(part)
        ref[rows, pl.ds(col, B)] = hi
        ref[rows, pl.ds(2 * B + col, B)] = hi
        ref[rows, pl.ds(4 * B + col, B)] = lo


def put_right(ref, real, imag):
    rh, rl = split(real)
    ih, il = split(imag)
    for base, r, i in ((0, rh, ih), (2 * B, rl, il), (4 * B, rh, ih)):
        for t in range(T):
            cut = slice(128 * t, 128 * (t + 1))
            ref[pl.ds(base, B), pl.ds(256 * t, 128)] = r[:, cut]
            ref[pl.ds(base, B), pl.ds(256 * t + 128, 128)] = i[:, cut]
            ref[pl.ds(base + B, B), pl.ds(256 * t, 128)] = -i[:, cut]
            ref[pl.ds(base + B, B), pl.ds(256 * t + 128, 128)] = r[:, cut]


def parts_of(wide):
    real = jnp.concatenate([wide[:, 256 * t : 256 * t + 128] for t in range(T)], axis=1)
    imag = jnp.concatenate([wide[:, 256 * t + 128 : 256 * t + 256] for t in range(T)], axis=1)
    return real, imag


def newton_but_last(k, matrix, approx, left, right, xr, xi):
    row = lax.broadcasted_iota(jnp.int32, (B, B), 0)
    col = lax.broadcasted_iota(jnp.int32, (B, B), 1)
    eye = row == col
    one = jnp.where(eye, 1.0, 0.0).astype(F32)
    cr = approx[0, pl.ds(k, 1), :]
    ci = approx[1, pl.ds(k, 1), :]
    cr_col = jnp.sum(jnp.where(eye, cr, 0.0), axis=1, keepdims=True)
    ci_col = jnp.sum(jnp.where(eye, ci, 0.0), axis=1, keepdims=True)
    mr = matrix[k, 0]
    mi = matrix[k, 1]
    yr = one - (mr * cr - mi * ci)
    yi = -(mr * ci + mi * cr)
    put_left(left, yr, yi, 0)
    put_right(right, yr, yi)
    ar = one + yr
    xr[...] = cr_col * ar - ci_col * yi
    xi[...] = cr_col * yi + ci_col * ar
    y0 = jnp.dot(left[pl.ds(0, B), :], right[...], preferred_element_type=F32)
    y0r, y0i = parts_of(y0)
    put_left(left, y0r, y0i, B)
    put_left(left, xr[...], xi[...], 0)
    put_right(right, y0r, y0i)
    both = jnp.dot(left[...], right[...], preferred_element_type=F32)
    dr, di = parts_of(both[:B])
    y1r, y1i = parts_of(both[B:])
    x1r = xr[...] + dr
    x1i = xi[...] + di
    xr[...] = x1r
    xi[...] = x1i
    put_left(left, x1r, x1i, 0)
    put_right(right, y1r, y1i)


def newton_last(k, t, left, right, xr, xi, lin):
    last = jnp.dot(left[pl.ds(0, B), :], right[:, pl.ds(256 * t, 256)], preferred_element_type=F32)
    cols = pl.ds(128 * t, 128)
    lin[k, t, 0] = xr[:, cols] + last[:, :128]
    lin[k, t, 1] = xi[:, cols] + last[:, 128:]


def here():
    return {a: lax.axis_index(a) for a in AXES}


def ring_z(me, n):
    side = (2 * lax.rem(n, 2) - 1) * (1 - 2 * me["c"])
    z = lax.rem(me["zh"] * 4 + me["zl"] + 4 + side * (n // 2), 8)
    return z, (lax.rem(z, 4), me["x"], me["y"], me["c"], z // 4)


def far_first(n):
    late = n // 2
    return (1 - late) * (2 - n) + late * lax.rem(n + 1, 4)


def plane(me, i):
    n = i - 1
    x = lax.rem(me["x"] + far_first(n // 8), 4)
    y = lax.rem(me["y"] + far_first(lax.rem(n // 2, 4)), 4)
    c = lax.rem(me["c"] + 1 - lax.rem(n, 2), 2)
    return (x * 4 + y) * 2 + c, (me["zl"], x, y, c, me["zh"])


def greet(me):
    barrier = pltpu.get_barrier_semaphore()

    def along_z(d, carry):
        pl.semaphore_signal(barrier, inc=1, device_id=ring_z(me, d)[1], device_id_type=MESH_ID)
        return carry

    def in_plane(i, carry):
        pl.semaphore_signal(barrier, inc=1, device_id=plane(me, i)[1], device_id_type=MESH_ID)
        return carry

    lax.fori_loop(1, 8, along_z, 0)
    lax.fori_loop(1, 32, in_plane, 0)
    return barrier


def send(src, dst, ssem, rsem, device):
    pltpu.make_async_remote_copy(
        src_ref=src, dst_ref=dst, send_sem=ssem, recv_sem=rsem, device_id=device, device_id_type=MESH_ID
    ).start()


def wait_for(ref, sem):
    pltpu.make_async_copy(ref, ref, sem).wait()


def step_kernel(
    matrix_hbm, approx_hbm, weight_hbm, shift_hbm, pairing_hbm, coupling_hbm, energy_hbm, force_hbm,
    green_hbm, sigma_hbm, force,
    approx, weight, shift, pairing, coupling, energy_weight, force_weight, small_sem, lin, out,
    matrix, left, right, xr, xi, zb, pb, cb, rb, kmat, shifted, xs, fleft, fright, fa, fb, near, own, far,
    ms, zs, zr, ps, pr, bs, br, ws, wr, ns, nr, fs, fr, gs, ss,
):
    me = here()
    my_z = me["zh"] * 4 + me["zl"]
    my_p = (me["x"] * 4 + me["y"]) * 2 + me["c"]
    mine = pl.ds(3 * my_p, 3)
    my_rows = pl.ds(pl.multiple_of(96 * me["zl"], 8), 96)

    loads = [pltpu.make_async_copy(matrix_hbm.at[:, 0, k], matrix.at[k], ms.at[k]) for k in range(2)]
    small = [
        pltpu.make_async_copy(src, dst, small_sem.at[n])
        for n, (src, dst) in enumerate(
            (
                (approx_hbm, approx),
                (weight_hbm, weight),
                (shift_hbm, shift),
                (pairing_hbm, pairing),
                (coupling_hbm, coupling),
                (energy_hbm, energy_weight),
                (force_hbm, force_weight),
            )
        )
    ]
    for load in small + loads:
        load.start()
    barrier = greet(me)

    def green_out(k, t, part):
        place = green_hbm.at[part, 0, k, :, pl.ds(128 * t, 128)]
        return pltpu.make_async_copy(lin.at[k, t, part], place, gs.at[k, t, part])

    def sigma_out(k, t, part):
        place = sigma_hbm.at[part, 0, k, :, pl.ds(128 * t, 128)]
        return pltpu.make_async_copy(out.at[t, k, part], place, ss.at[k, t, part])

    def z_forward(k, t):
        def along_z(d, carry):
            z, device = ring_z(me, d)
            rows = pl.ds(pl.multiple_of(96 * lax.rem(z, 4), 8), 96)
            send(lin.at[k, t, z // 4, rows], zb.at[k, t, my_z], zs.at[k, t], zr.at[k, t], device)
            return carry

        lax.fori_loop(1, 8, along_z, 0)
        pltpu.make_async_copy(lin.at[k, t, me["zh"], my_rows], zb.at[k, t, my_z], zr.at[k, t]).start()

    def plane_forward(k, t):
        wait_for(zb.at[k, t], zr.at[k, t])

        def in_plane(i, carry):
            p, device = plane(me, i)
            send(zb.at[k, t, :, pl.ds(3 * p, 3)], pb.at[k, t, :, mine], ps.at[k, t], pr.at[k, t], device)
            return carry

        lax.fori_loop(1, 32, in_plane, 0)
        pltpu.make_async_copy(zb.at[k, t, :, mine], pb.at[k, t, :, mine], pr.at[k, t]).start()

    def plane_back(k, t):
        def in_plane(i, carry):
            p, device = plane(me, i)
            send(cb.at[t, k, :, pl.ds(3 * p, 3)], rb.at[t, k, :, mine], bs.at[t, k], br.at[t, k], device)
            return carry

        lax.fori_loop(1, 32, in_plane, 0)
        pltpu.make_async_copy(cb.at[t, k, :, mine], rb.at[t, k, :, mine], br.at[t, k]).start()

    def z_back(k, t):
        wait_for(rb.at[t, k], br.at[t, k])

        def along_z(d, carry):
            z, device = ring_z(me, d)
            send(rb.at[t, k, z], out.at[t, k, me["zh"], my_rows], ws.at[t, k], wr.at[t, k], device)
            return carry

        lax.fori_loop(1, 8, along_z, 0)
        pltpu.make_async_copy(rb.at[t, k, my_z], out.at[t, k, me["zh"], my_rows], wr.at[t, k]).start()

    def build_kernel():
        e = lax.broadcasted_iota(jnp.int32, (128, 128), 0)
        f = lax.broadcasted_iota(jnp.int32, (128, 128), 1)
        for q in range(4):
            total = jnp.zeros((128, 128), F32)
            for m in range(6):
                total = total + jnp.where(f == e - shift[q, m], weight[q, m], 0.0)
            shifted[q] = total
        for kk in range(4):
            for ll in range(4):
                block = jnp.zeros((128, 128), F32)
                for q in range(4):
                    same = (e * 0 + pairing[kk, q]) == ll
                    block = block + jnp.where(same, shifted[q], 0.0)
                hi, lo = split(block)
                row = pl.ds(128 * ((kk % 2) * 2 + kk // 2), 128)
                col = 128 * ((ll % 2) * 2 + ll // 2)
                kmat[row, pl.ds(col, 128)] = hi
                kmat[row, pl.ds(512 + col, 128)] = hi
                kmat[row, pl.ds(1024 + col, 128)] = lo

    def convolve(t):
        for k in range(2):
            wait_for(pb.at[k, t], pr.at[k, t])
            for z in range(8):
                rows = pl.ds(256 * k + 32 * z, 32)
                for j in range(3):
                    hi, lo = split(pb[k, t, z, pl.ds(j, 32, stride=3), :])
                    cols = pl.ds(128 * j, 128)
                    xs[rows, cols] = hi
                    xs[pl.ds(512 + 256 * k + 32 * z, 32), cols] = lo
                    xs[pl.ds(1024 + 256 * k + 32 * z, 32), cols] = hi
        for k in range(2):
            result = jnp.dot(kmat[pl.ds(256 * k, 256), :], xs[...], preferred_element_type=F32)
            for j in range(3):
                scaled = result[:, 128 * j : 128 * (j + 1)] * coupling[pl.ds(j, 1), pl.ds(128 * t, 128)]
                for z in range(8):
                    cb[t, k, z, pl.ds(j, 32, stride=3), :] = scaled[32 * z : 32 * z + 32, :]
            plane_back(k, t)

    def build_force_left():
        for k in range(2):
            for part in range(2):
                for t in range(T):
                    hi, lo = split(lin[k, t, part])
                    for term, value in ((0, hi), (1, hi), (2, lo)):
                        fleft[k, :, pl.ds((2 * term + part) * B + 128 * t, 128)] = value

    def force_term(t, k):
        wait_for(out.at[t, k], wr.at[t, k])
        for part in range(2):
            sigma_out(k, t, part).start()
            s = out[t, k, part]
            hi, lo = split(s if part == 0 else -s)
            for term, value in ((0, hi), (1, lo), (2, hi)):
                fright[pl.ds((2 * term + part) * B, B), :] = value
        return jnp.dot(fleft[k], fright[...], preferred_element_type=F32)

    def force_part(t):
        fa[...] = force_term(t, 0)
        fa[...] = (fa[...] + force_term(t, 1)) * energy_weight[0]
        for z in range(4):
            for j in range(3):
                fb[t, pl.ds(3 * z + j, 32, stride=12), :] = fa[pl.ds(96 * z + j, 32, stride=3), :]

        def in_plane(i, carry):
            p, device = plane(me, i)
            send(fb.at[t, pl.ds(12 * p, 12)], near.at[t, pl.ds(12 * my_p, 12)], ns.at[t], nr.at[t], device)
            return carry

        lax.fori_loop(1, 32, in_plane, 0, unroll=True)
        own_rows = pl.ds(12 * my_p, 12)
        pltpu.make_async_copy(fb.at[t, own_rows], near.at[t, own_rows], nr.at[t]).start()

    def force_along_z(t):
        wait_for(near.at[t], nr.at[t])
        total = near[t, pl.ds(0, 24), :]
        for p in range(1, 16):
            total = total + near[t, pl.ds(24 * p, 24), :]
        own[t] = total[:12] + total[12:]

        def along_z(d, carry):
            z, device = ring_z(me, d)
            send(own.at[t, pl.ds(3 * lax.rem(z, 4), 3)], far.at[t, pl.ds(3 * my_z, 3)], fs.at[t], fr.at[t], device)
            return carry

        lax.fori_loop(1, 8, along_z, 0, unroll=True)
        own_rows = own.at[t, pl.ds(3 * me["zl"], 3)]
        pltpu.make_async_copy(own_rows, far.at[t, pl.ds(3 * my_z, 3)], fr.at[t]).start()

    def force_out(t):
        wait_for(far.at[t], fr.at[t])
        total = far[t, pl.ds(0, 3), :]
        for z in range(1, 8):
            total = total + far[t, pl.ds(3 * z, 3), :]
        cols = pl.ds(128 * t, 128)
        force[:, cols] = total * force_weight[:, cols]

    for load in small:
        load.wait()
    loads[0].wait()
    newton_but_last(0, matrix, approx, left, right, xr, xi)
    pl.semaphore_wait(barrier, 38)
    for t in range(T):
        newton_last(0, t, left, right, xr, xi, lin)
        if t < 1:
            z_forward(0, t)
    loads[1].wait()
    newton_but_last(1, matrix, approx, left, right, xr, xi)
    for t in range(T):
        newton_last(1, t, left, right, xr, xi, lin)
        z_forward(1, t)
        if t < 2:
            z_forward(0, t + 1)
    for k in range(2):
        for t in range(T):
            for part in range(2):
                green_out(k, t, part).start()
    plane_forward(0, 0)
    build_kernel()
    plane_forward(1, 0)
    convolve(0)
    plane_forward(0, 1)
    plane_forward(1, 1)
    z_back(0, 0)
    z_back(1, 0)
    convolve(1)
    build_force_left()
    plane_forward(0, 2)
    z_back(0, 1)
    z_back(1, 1)
    plane_forward(1, 2)
    convolve(2)
    z_back(0, 2)
    z_back(1, 2)
    force_part(0)
    force_part(1)
    force_along_z(0)
    force_along_z(1)
    force_part(2)
    force_along_z(2)
    for t in range(T):
        force_out(t)

    for t in range(T):
        for k in range(2):
            for part in range(2):
                green_out(k, t, part).wait()
                sigma_out(k, t, part).wait()
            wait_for(zb.at[k, t, pl.ds(0, 7)], zs.at[k, t])
            wait_for(pb.at[k, t, :, pl.ds(0, 93)], ps.at[k, t])
            wait_for(rb.at[t, k, :, pl.ds(0, 93)], bs.at[t, k])
            wait_for(rb.at[t, k, pl.ds(0, 7)], ws.at[t, k])
        wait_for(near.at[t, pl.ds(0, 372)], ns.at[t])
        wait_for(far.at[t, pl.ds(0, 21)], fs.at[t])


def step(matrix, approx, weight, shift, pairing, coupling, energy_weight, force_weight):
    dma = pltpu.SemaphoreType.DMA
    return pl.pallas_call(
        step_kernel,
        out_shape=(
            jax.ShapeDtypeStruct((2, 1, 2, B, B), F32),
            jax.ShapeDtypeStruct((2, 1, 2, B, B), F32),
            jax.ShapeDtypeStruct((3, B), F32),
        ),
        in_specs=[pl.BlockSpec(memory_space=pltpu.HBM)] * 8,
        out_specs=(pl.BlockSpec(memory_space=pltpu.HBM), pl.BlockSpec(memory_space=pltpu.HBM), VMEM),
        scratch_shapes=[
            pltpu.VMEM((2, 2, B), F32),
            pltpu.SMEM((4, 6), F32),
            pltpu.SMEM((4, 6), jnp.int32),
            pltpu.SMEM((4, 4), jnp.int32),
            pltpu.VMEM((3, B), F32),
            pltpu.SMEM((1,), F32),
            pltpu.VMEM((3, B), F32),
            dma((7,)),
            pltpu.VMEM((2, T, 2, B, 128), F32),
            pltpu.VMEM((T, 2, 2, B, 128), F32),
            pltpu.VMEM((2, 2, B, B), F32),
            pltpu.VMEM((2 * B, 6 * B), BF16),
            pltpu.VMEM((6 * B, 2 * B), BF16),
            pltpu.VMEM((B, B), F32),
            pltpu.VMEM((B, B), F32),
            pltpu.VMEM((2, T, 8, 96, 128), F32),
            pltpu.VMEM((2, T, 8, 96, 128), F32),
            pltpu.VMEM((T, 2, 8, 96, 128), F32),
            pltpu.VMEM((T, 2, 8, 96, 128), F32),
            pltpu.VMEM((512, 1536), BF16),
            pltpu.VMEM((4, 128, 128), F32),
            pltpu.VMEM((1536, 384), BF16),
            pltpu.VMEM((2, B, 6 * B), BF16),
            pltpu.VMEM((6 * B, 128), BF16),
            pltpu.VMEM((B, 128), F32),
            pltpu.VMEM((T, B, 128), F32),
            pltpu.VMEM((T, B, 128), F32),
            pltpu.VMEM((T, 12, 128), F32),
            pltpu.VMEM((T, 24, 128), F32),
            dma((2,)),
            dma((2, T)), dma((2, T)),
            dma((2, T)), dma((2, T)),
            dma((T, 2)), dma((T, 2)),
            dma((T, 2)), dma((T, 2)),
            dma((T,)), dma((T,)),
            dma((T,)), dma((T,)),
            dma((2, T, 2)), dma((2, T, 2)),
        ],
        compiler_params=pltpu.CompilerParams(
            collective_id=1, has_side_effects=True, vmem_limit_bytes=67043328
        ),
        name="step",
    )(matrix, approx, weight, shift, pairing, coupling, energy_weight, force_weight)


def copy_kernel(green, sigma, force, green_out, sigma_out, force_out, held, arrived, left):
    moves = []
    for n, (src, dst) in enumerate(((green, green_out), (sigma, sigma_out))):
        for part in range(2):
            for k in range(2):
                for h in range(CUT):
                    rows = pl.ds(h * (B // CUT), B // CUT)
                    m = len(moves)
                    place = held.at[n, part, k, rows]
                    moves.append((
                        pltpu.make_async_copy(src.at[part, 0, k, rows], place, arrived.at[m]),
                        pltpu.make_async_copy(place, dst.at[part, 0, k, rows], left.at[m]),
                    ))
    for inward, _ in moves:
        inward.start()
    force_out[...] = force[...]
    for inward, outward in moves:
        inward.wait()
        outward.start()
    for _, outward in moves:
        outward.wait()


CUT = 2


def final_copies(green, sigma, force):
    hbm = pl.BlockSpec(memory_space=pltpu.HBM)
    large = jax.ShapeDtypeStruct((2, 1, 2, B, B), F32)
    return pl.pallas_call(
        copy_kernel,
        out_shape=(large, large, jax.ShapeDtypeStruct((3, B), F32)),
        in_specs=[hbm, hbm, VMEM],
        out_specs=(hbm, hbm, VMEM),
        scratch_shapes=[
            pltpu.VMEM((2, 2, 2, B, B), F32),
            pltpu.SemaphoreType.DMA((8 * CUT,)),
            pltpu.SemaphoreType.DMA((8 * CUT,)),
        ],
        compiler_params=pltpu.CompilerParams(vmem_limit_bytes=67043328),
        name="copies",
    )(green, sigma, force)


def per_device(
    system_matrix, approx_inverse, mode_weight, phonon_shift, pairing, coupling, energy_weight, force_weight
):
    green, sigma, force = step(
        system_matrix, approx_inverse.reshape(2, 2, B), mode_weight, phonon_shift, pairing, coupling,
        energy_weight, force_weight,
    )
    return final_copies(green, sigma, force)


def solution(mesh):
    torus = Mesh(mesh.devices.reshape(4, 4, 4, 2, 2), AXES)
    return jax.shard_map(
        per_device,
        mesh=torus,
        in_specs=(
            P(None, ENERGY, "zh", None, None),
            P(None, ENERGY, "zh", None),
            P(),
            P(),
            P(),
            P(ENERGY, None),
            P(ENERGY),
            P(ENERGY, None),
        ),
        out_specs=(
            P(None, ENERGY, "zh", None, None),
            P(None, ENERGY, "zh", None, None),
            P(ENERGY, None),
        ),
        check_vma=False,
    )
```
